256 devices in a mesh: gx: 8 (over x_lo, y), gy: 32 (over z, x_hi, core).
Axes of the slice: x: 4 (x_hi: 2, x_lo: 2; x = x_hi * 2 + x_lo), y: 4, z: 8, core: 2. Of those that a mesh axis runs over, the one named last changes fastest.
Arguments:
- plan: int32 [44], replicated, may hold values from 0 to 43, each once
- amplitude: float32 [8, 32, 44, 2, 128], P('gx', 'gy'), may hold values from -12 to 12
- positions: int32 [8, 32, 44, 128], P('gx', 'gy'), may hold values from 0 to 1023
- west_in: bfloat16 [8, 32, 2, 128, 1024], P('gx', 'gy'), may hold values from -6 to 6
- north_in: bfloat16 [8, 32, 2, 128, 1024], P('gx', 'gy'), may hold values from -6 to 6
- corner_now: bfloat16 [8, 32, 2, 128, 128], P('gx', 'gy'), may hold values from -6 to 6
- corner_next: bfloat16 [8, 32, 2, 128, 128], P('gx', 'gy'), may hold values from -6 to 6
- east_map: bfloat16 [8, 32, 2, 1024, 1024], P('gx', 'gy'), may hold values from -0.09375 to 0.09375
- south_map: bfloat16 [8, 32, 2, 1024, 1024], P('gx', 'gy'), may hold values from -0.09375 to 0.09375
Outputs:
- west_out: bfloat16 [8, 32, 2, 128, 1024], P('gx', 'gy')
- north_out: bfloat16 [8, 32, 2, 128, 1024], P('gx', 'gy')
- corner_first: bfloat16 [8, 32, 2, 128, 128], P('gx', 'gy')
- corner_second: bfloat16 [8, 32, 2, 128, 128], P('gx', 'gy')
- interface_residual: float32 [8, 32, 2, 128, 1024], P('gx', 'gy')
The draws below stay inside these ranges and needn't reach their ends.
Inputs may be any that keep to these rules, and one draw needn't show every extreme that they name: `plan`: a permutation of the 44 batches.
All inputs are finite; a program needn't handle non-finite values.
Results may differ from the reference program's by a relative error of at most 0.015.
Values may be sent and summed in bfloat16 or wider, within the bound.
A program may use at most 64 MiB of HBM per device.

```python
import jax
import jax.numpy as jnp
from jax import lax

M = 1024
K = 128
S = 128
TICKS = 6
NX = 8
NY = 32
NB = 44


def with_ends(array, rng, least, high):
    extent = array.shape
    place = [jax.random.randint(jax.random.fold_in(rng, axis), (), 0, extent[axis]) for axis in range(len(extent))]
    array = array.at[tuple(place)].set(least)
    longest = extent.index(max(extent))
    place[longest] = (place[longest] + 1) % extent[longest]
    return array.at[tuple(place)].set(high)


def block_levels(key, extent, pieces, smallest, high):
    def one(position, parts):
        heights = jax.random.uniform(jax.random.fold_in(jax.random.fold_in(key, 6), position), (parts,), jnp.float32, smallest / len(pieces), high / len(pieces))
        return jnp.repeat(jnp.exp(heights), extent[position] // parts).reshape((-1,) + (1,) * (len(extent) - position - 1))

    factor_of = one(*pieces[0])
    for cut in pieces[1:]:
        factor_of = factor_of * one(*cut)
    return factor_of


def bell_draw(stream_key, dims, width, bound, cuts=(), kind=jnp.bfloat16):
    level = block_levels(stream_key, dims, cuts, -0.22, 0.18) if cuts else 1.0
    entries = jax.random.normal(stream_key, dims, jnp.float32) * width * level
    return jnp.minimum(jnp.maximum(entries, -bound), bound).astype(kind)


def setup_inputs(seed: int = 0) -> dict:
    key_list = jax.random.split(jax.random.key(seed), 10)
    plan = jax.random.permutation(key_list[0], NB).astype(jnp.int32)
    amplitude = bell_draw(key_list[1], (NX, NY, NB, 2, S), 2.0, 12.0, ((0, 8), (1, 32)), jnp.float32)
    positions = with_ends(jax.random.randint(key_list[2], (NX, NY, NB, S), 0, M), jax.random.fold_in(key_list[2], 1), 0, M - 1).astype(jnp.int32)
    west_in = bell_draw(key_list[3], (NX, NY, 2, S, M), 1.0, 6.0, ((0, 8), (1, 32)))
    north_in = bell_draw(key_list[4], (NX, NY, 2, S, M), 1.0, 6.0, ((0, 8), (1, 32)))
    corner_now = bell_draw(key_list[5], (NX, NY, 2, S, K), 1.0, 6.0, ((0, 8), (1, 32)))
    corner_next = bell_draw(key_list[6], (NX, NY, 2, S, K), 1.0, 6.0, ((0, 8), (1, 32)))
    east_map = bell_draw(key_list[7], (NX, NY, 2, M, M), (4 * M) ** -0.5, 0.09375, ((0, 8), (1, 32)))
    south_map = bell_draw(key_list[8], (NX, NY, 2, M, M), (4 * M) ** -0.5, 0.09375, ((0, 8), (1, 32)))
    return {"plan": plan, "amplitude": amplitude, "positions": positions, "west_in": west_in, "north_in": north_in, "corner_now": corner_now, "corner_next": corner_next, "east_map": east_map, "south_map": south_map}


def apply_row(boundary, maps):
    values = boundary.astype(jnp.float32)
    mats = maps.astype(jnp.float32)
    real = jnp.einsum("ysm,ymn->ysn", values[:, 0], mats[:, 0]) - jnp.einsum("ysm,ymn->ysn", values[:, 1], mats[:, 1])
    imag = jnp.einsum("ysm,ymn->ysn", values[:, 0], mats[:, 1]) + jnp.einsum("ysm,ymn->ysn", values[:, 1], mats[:, 0])
    return jnp.stack([real, imag], 1).astype(jnp.bfloat16)


def push_east(field):
    return jnp.concatenate([jnp.zeros_like(field[:1]), field[:-1]], 0)


def push_south(field):
    return jnp.concatenate([jnp.zeros_like(field[:, :1]), field[:, :-1]], 1)


def reference(plan, amplitude, positions, west_in, north_in, corner_now, corner_next, east_map, south_map):
    west, north = west_in, north_in
    corner_a, corner_b = corner_now, corner_next
    column = lax.broadcasted_iota(jnp.int32, (NX, NY), 0)
    row = lax.broadcasted_iota(jnp.int32, (NX, NY), 1)
    boundary = None
    for tick in range(TICKS):
        slot = (tick - column - row + NX + NY - 2).astype(jnp.int32)
        batch = plan[slot]
        amps = jnp.take_along_axis(amplitude, batch[:, :, None, None, None], axis=2)[:, :, 0]
        places = jnp.take_along_axis(positions, batch[:, :, None, None], axis=2)[:, :, 0]
        points = lax.broadcasted_iota(jnp.int32, (NX, NY, S, M), 3)
        onehot = (points == places[:, :, :, None]).astype(jnp.float32)
        total = west.astype(jnp.float32) + north.astype(jnp.float32) + amps[:, :, :, :, None] * onehot[:, :, None]
        padded_corner = jnp.pad(corner_a.astype(jnp.float32), ((0, 0), (0, 0), (0, 0), (0, 0), (0, M - K)))
        boundary = (total + padded_corner).astype(jnp.bfloat16)
        east_out = lax.map(lambda pair: apply_row(pair[0], pair[1]), (boundary, east_map))
        south_out = lax.map(lambda pair: apply_row(pair[0], pair[1]), (boundary, south_map))
        west = push_east(east_out)
        north = push_south(south_out)
        corner_a = corner_b
        corner_b = push_south(push_east(east_out[..., :K]))
    values = boundary.astype(jnp.float32)
    padded = jnp.pad(values, ((1, 1), (1, 1), (0, 0), (0, 0), (0, 0)))
    residual = 4.0 * values - padded[:-2, 1:-1] - padded[2:, 1:-1] - padded[1:-1, :-2] - padded[1:-1, 2:]
    return west, north, corner_a, corner_b, residual
```

```python
import functools

import jax
import jax.numpy as jnp
from jax import lax
from jax.experimental import pallas as pl
from jax.experimental.pallas import tpu as pltpu
from jax.sharding import PartitionSpec as P

MESH = pl.DeviceIdType.MESH
TICKS = 6
GROUPS = 4
LAG = 2
BF16 = jnp.bfloat16
F32 = jnp.float32


def kernel(
    nx,
    ny,
    plan,
    amp_hbm,
    pos_hbm,
    west_hbm,
    north_hbm,
    now_hbm,
    next_hbm,
    east_hbm,
    south_hbm,
    west_out,
    north_out,
    first_out,
    second_out,
    resid_out,
    amp,
    pos,
    maps,
    wbuf,
    nbuf,
    cbuf,
    ebuf,
    fbuf,
    qbuf,
    rbuf,
    relay,
    c1buf,
    c2buf,
    resid,
    rows_s,
    cols_s,
    small_sem,
    map_sem,
    c_sem,
    w_sem,
    n_sem,
    es_sem,
    fs_sem,
    rl_sem,
    rs_sem,
    q_send,
    q_recv,
    k_send,
    k_recv,
    out_sem,
):
    gx = lax.axis_index("gx")
    gy = lax.axis_index("gy")
    G = GROUPS
    R = west_hbm.shape[3] // G
    M = west_hbm.shape[4]
    K = now_hbm.shape[4]
    NC = min(256, M)
    half = nx // 2
    has_w = gx > 0
    has_e = gx < nx - 1
    has_n = gy > 0
    has_s = gy < ny - 1
    east = (gx + 1, gy)
    west = (gx - 1, gy)
    south = (gx, gy + 1)
    north = (gx, gy - 1)
    giver = gx == half - 1
    hub = gx == 0
    taker = gx == half
    hub_dev = (0, gy)
    giver_dev = (half - 1, gy)
    taker_dev = (half, gy)

    barrier = pltpu.get_barrier_semaphore()
    partners = (
        (has_e, east),
        (has_w, west),
        (has_s, south),
        (has_n, north),
        (giver, hub_dev),
        (hub, giver_dev),
        (hub, taker_dev),
        (taker, hub_dev),
    )
    for cond, dev in partners:

        @pl.when(cond)
        def _():
            pl.semaphore_signal(barrier, 1, device_id=dev, device_id_type=MESH)

    amp_copy = pltpu.make_async_copy(amp_hbm.at[0, 0], amp, small_sem.at[0])
    pos_copy = pltpu.make_async_copy(pos_hbm.at[0], pos, small_sem.at[1])
    amp_copy.start()
    pos_copy.start()

    def rows_of(g):
        return pl.ds(g * R, R)

    for g in range(G):
        pltpu.make_async_copy(west_hbm.at[0, 0, :, rows_of(g)], wbuf.at[g], w_sem.at[g]).start()
        pltpu.make_async_copy(north_hbm.at[0, 0, :, rows_of(g)], nbuf.at[g], n_sem.at[g]).start()
    corner_copies = []
    for k, ref in enumerate((now_hbm, next_hbm)):
        for g in range(G):
            corner_copies.append(
                pltpu.make_async_copy(
                    ref.at[0, 0, :, rows_of(g)], cbuf.at[k * G + g], c_sem.at[k * G + g]
                )
            )
    for c in corner_copies:
        c.start()
    map_copies = []
    for k, ref in enumerate((east_hbm, south_hbm)):
        for c in range(2):
            map_copies.append(
                pltpu.make_async_copy(ref.at[0, 0, c], maps.at[k, c], map_sem.at[k * 2 + c])
            )
    for c in map_copies:
        c.start()

    ZW = (TICKS + 1) * G
    wbuf[ZW] = jnp.zeros((2, R, M), BF16)
    nbuf[ZW] = jnp.zeros((2, R, M), BF16)
    ZR = 4 * G
    rbuf[ZR] = jnp.zeros((2, R, M), BF16)

    rows_s[...] = jnp.zeros_like(rows_s)
    amp_copy.wait()
    pos_copy.wait()
    for t in range(TICKS):
        b = plan[t - gx - gy + nx + ny - 2]
        rows_s[8 * t : 8 * t + 2, :] = amp[b]
        rows_s[8 * t + 2 : 8 * t + 3, :] = pos[b].astype(F32)
    flipped = rows_s[...].T
    for t in range(TICKS):
        cols_s[t] = flipped[:, 8 * t : 8 * t + 8]

    def w_index(t, g):
        return jnp.where(hub & (t > 0), ZW, t * G + g)

    def n_index(t, g):
        return jnp.where((gy == 0) & (t > 0), ZW, t * G + g)

    def w_copy(t, g, dev):
        it = t * G + g
        return pltpu.make_async_remote_copy(
            ebuf.at[it],
            wbuf.at[it + G],
            es_sem.at[it],
            w_sem.at[it + G],
            device_id=dev,
            device_id_type=MESH,
        )

    def hub_copy(t, g):
        it = t * G + g
        k = t * (G // 2) + g // 2
        return pltpu.make_async_remote_copy(
            ebuf.at[it],
            relay.at[k],
            es_sem.at[it],
            rl_sem.at[k],
            device_id=hub_dev,
            device_id_type=MESH,
        )

    def onward_copy(t, g):
        it = t * G + g
        k = t * (G // 2) + g // 2
        return pltpu.make_async_remote_copy(
            relay.at[k],
            wbuf.at[it + G],
            rs_sem.at[k],
            w_sem.at[it + G],
            device_id=taker_dev,
            device_id_type=MESH,
        )

    def n_copy(t, g):
        it = t * G + g
        return pltpu.make_async_remote_copy(
            fbuf.at[it],
            nbuf.at[it + G],
            fs_sem.at[it],
            n_sem.at[it + G],
            device_id=south,
            device_id_type=MESH,
        )

    def q_copy(d, g, dev):
        return pltpu.make_async_remote_copy(
            qbuf.at[g],
            rbuf.at[d * G + g],
            q_send.at[d * G + g],
            q_recv.at[d * G + g],
            device_id=dev,
            device_id_type=MESH,
        )

    KQ = TICKS * (G // 2)

    def q_hub_copy(g):
        k = KQ + g // 2
        return pltpu.make_async_remote_copy(
            qbuf.at[g],
            relay.at[k],
            q_send.at[3 * G + g],
            rl_sem.at[k],
            device_id=hub_dev,
            device_id_type=MESH,
        )

    def q_onward_copy(g):
        k = KQ + g // 2
        return pltpu.make_async_remote_copy(
            relay.at[k],
            rbuf.at[3 * G + g],
            rs_sem.at[k],
            q_recv.at[3 * G + g],
            device_id=taker_dev,
            device_id_type=MESH,
        )

    def corner_copy(which, g):
        t = TICKS - 1 + which
        dst = (c1buf, c2buf)[which]
        return pltpu.make_async_remote_copy(
            wbuf.at[w_index(t, g), :, :, pl.ds(0, K)],
            dst.at[g],
            k_send.at[which * G + g],
            k_recv.at[which * G + g],
            device_id=south,
            device_id_type=MESH,
        )

    lanes = lax.broadcasted_iota(jnp.int32, (R, NC), 1).astype(F32)

    def step(it, carry):
        t = it // G
        g = it % G
        odd = g % 2 == 1

        @pl.when(t == 0)
        def _():
            pltpu.make_async_copy(
                west_hbm.at[0, 0, :, pl.ds(pl.multiple_of(g * R, R), R)], wbuf.at[g], w_sem.at[g]
            ).wait()
            pltpu.make_async_copy(
                north_hbm.at[0, 0, :, pl.ds(pl.multiple_of(g * R, R), R)], nbuf.at[g], n_sem.at[g]
            ).wait()

        @pl.when((t > 0) & has_w)
        def _():
            w_copy(t - 1, g, east).wait_recv()

        @pl.when((t > 0) & has_n)
        def _():
            n_copy(t - 1, g).wait_recv()

        @pl.when(it == 0)
        def _():
            for c in corner_copies:
                c.wait()

        wi = w_index(t, g)
        ni = n_index(t, g)
        ci = jnp.minimum(t, 1) * G + g
        cols = cols_s[t, pl.ds(pl.multiple_of(g * R, R), R), :]
        place = cols[:, 2:3]
        for n0 in range(0, M, NC):
            hit = lanes == (place - n0)
            for c in range(2):
                total = wbuf[wi, c, :, n0 : n0 + NC].astype(F32) + nbuf[
                    ni, c, :, n0 : n0 + NC
                ].astype(F32)
                total = total + jnp.where(hit, cols[:, c : c + 1], 0.0)
                if n0 < K:
                    corner = jnp.where(t < 2, cbuf[ci, c].astype(F32), 0.0)
                    qbuf[g, c, :, 0:K] = (total[:, :K] + corner).astype(BF16)
                    if NC > K:
                        qbuf[g, c, :, K:NC] = total[:, K:].astype(BF16)
                else:
                    qbuf[g, c, :, n0 : n0 + NC] = total.astype(BF16)

        def apply(which, dst, fold):
            lhs = qbuf[g].reshape(2 * R, M)
            for n0 in range(0, M, NC):
                a = jnp.dot(lhs, maps[which, 0, :, n0 : n0 + NC], preferred_element_type=F32)
                b = jnp.dot(lhs, maps[which, 1, :, n0 : n0 + NC], preferred_element_type=F32)
                parts = (a[:R] - b[R:], b[:R] + a[R:])
                for c in range(2):
                    part = parts[c]
                    if fold and n0 < K:
                        carried = jnp.where(
                            (t > 0) & (t < TICKS - 1), wbuf[wi, c, :, 0:K].astype(F32), 0.0
                        )
                        dst[it, c, :, 0:K] = (part[:, :K] + carried).astype(BF16)
                        if NC > K:
                            dst[it, c, :, K:NC] = part[:, K:].astype(BF16)
                    else:
                        dst[it, c, :, n0 : n0 + NC] = part.astype(BF16)

        @pl.when(it == 0)
        def _():
            map_copies[0].wait()
            map_copies[1].wait()

        apply(0, ebuf, False)

        @pl.when(it == 0)
        def _():
            count = sum(cond.astype(jnp.int32) for cond, _ in partners)
            pl.semaphore_wait(barrier, count)
            map_copies[2].wait()
            map_copies[3].wait()

        @pl.when(has_e & jnp.logical_not(giver & odd))
        def _():
            w_copy(t, g, east).start()

        @pl.when(giver & odd)
        def _():
            hub_copy(t, g).start()

        @pl.when(t == TICKS - 1)
        def _():
            @pl.when(has_s)
            def _():
                corner_copy(0, g).start()
                q_copy(2, g, south).start()

            @pl.when(has_w)
            def _():
                q_copy(0, g, west).start()

            @pl.when(has_n)
            def _():
                q_copy(1, g, north).start()

        apply(1, fbuf, True)

        @pl.when(has_s)
        def _():
            n_copy(t, g).start()

        back = it - LAG

        @pl.when(hub & (back >= 0) & (back % 2 == 1))
        def _():
            bt = back // G
            bg = back % G
            hub_copy(bt, bg).wait_recv()
            onward_copy(bt, bg).start()

        return carry

    lax.fori_loop(0, TICKS * G, step, 0)

    last = TICKS - 1
    for g in range(G):
        if g % 2 == 1:

            @pl.when(giver)
            def _():
                q_hub_copy(g).start()

        @pl.when(has_e & jnp.logical_not(giver & (g % 2 == 1)))
        def _():
            q_copy(3, g, east).start()

    for back in range(TICKS * G - LAG, TICKS * G):
        if back % 2 == 1:

            @pl.when(hub)
            def _():
                hub_copy(back // G, back % G).wait_recv()
                onward_copy(back // G, back % G).start()

    outs = []

    def put(src, dst, k):
        copy = pltpu.make_async_copy(src, dst, out_sem.at[k])
        copy.start()
        outs.append(copy)

    for g in range(G):

        @pl.when(has_w)
        def _():
            w_copy(last, g, east).wait_recv()

        @pl.when(has_s)
        def _():
            corner_copy(1, g).start()

        put(wbuf.at[w_index(TICKS, g)], west_out.at[0, 0, :, rows_of(g)], g)

    for g in range(G):

        @pl.when(has_n)
        def _():
            n_copy(last, g).wait_recv()

        put(nbuf.at[n_index(TICKS, g)], north_out.at[0, 0, :, rows_of(g)], G + g)

    for which, dst, buf in ((0, first_out, c1buf), (1, second_out, c2buf)):
        for g in range(G):

            @pl.when(has_n)
            def _():
                corner_copy(which, g).wait_recv()

            @pl.when(jnp.logical_not(has_n))
            def _():
                buf[g] = jnp.zeros((2, R, K), BF16)

            put(buf.at[g], dst.at[0, 0, :, rows_of(g)], (2 + which) * G + g)

    for g in range(G):
        if g % 2 == 1:

            @pl.when(hub)
            def _():
                q_hub_copy(g).wait_recv()
                q_onward_copy(g).start()

    for g in range(G):
        sides = ((has_e, 0, west), (has_s, 1, north), (has_n, 2, south), (has_w, 3, east))
        for cond, d, dev in sides:

            @pl.when(cond)
            def _():
                q_copy(d, g, dev).wait_recv()

        idx = [jnp.where(cond, d * G + g, ZR) for cond, d, _ in sides]
        for n0 in range(0, M, NC):
            cut = slice(n0, n0 + NC)
            for c in range(2):
                value = 4.0 * qbuf[g, c, :, cut].astype(F32)
                for i in (3, 0, 2, 1):
                    value = value - rbuf[idx[i], c, :, cut].astype(F32)
                resid[g, c, :, cut] = value
        put(resid.at[g], resid_out.at[0, 0, :, rows_of(g)], 4 * G + g)

    def drain(it, carry):
        t = it // G
        g = it % G
        odd = g % 2 == 1

        @pl.when(has_e & jnp.logical_not(giver & odd))
        def _():
            w_copy(t, g, east).wait_send()

        @pl.when(giver & odd)
        def _():
            hub_copy(t, g).wait_send()

        @pl.when(has_s)
        def _():
            n_copy(t, g).wait_send()

        @pl.when(hub & odd)
        def _():
            onward_copy(t, g).wait_send()

        return carry

    lax.fori_loop(0, TICKS * G, drain, 0)
    for g in range(G):

        @pl.when(has_s)
        def _():
            corner_copy(0, g).wait_send()
            corner_copy(1, g).wait_send()
            q_copy(2, g, south).wait_send()

        @pl.when(has_w)
        def _():
            q_copy(0, g, west).wait_send()

        @pl.when(has_n)
        def _():
            q_copy(1, g, north).wait_send()

        if g % 2 == 1:

            @pl.when(giver)
            def _():
                q_hub_copy(g).wait_send()

            @pl.when(hub)
            def _():
                q_onward_copy(g).wait_send()

        @pl.when(has_e & jnp.logical_not(giver & (g % 2 == 1)))
        def _():
            q_copy(3, g, east).wait_send()

    for copy in outs:
        copy.wait()


def solution(mesh):
    nx, ny = mesh.shape["gx"], mesh.shape["gy"]

    def step(plan, amplitude, positions, west, north, now, nxt, east_map, south_map):
        G = GROUPS
        S, M = west.shape[3], west.shape[4]
        K = now.shape[4]
        R = S // G
        hbm = pl.BlockSpec(memory_space=pl.ANY)
        cell = (2, R, M)
        tick_cells = TICKS * G
        out_shape = (
            jax.ShapeDtypeStruct(west.shape, BF16),
            jax.ShapeDtypeStruct(north.shape, BF16),
            jax.ShapeDtypeStruct(now.shape, BF16),
            jax.ShapeDtypeStruct(nxt.shape, BF16),
            jax.ShapeDtypeStruct(west.shape, F32),
        )
        dma = pltpu.SemaphoreType.DMA
        n_relay = (TICKS + 1) * G // 2
        return pl.pallas_call(
            functools.partial(kernel, nx, ny),
            out_shape=out_shape,
            in_specs=[pl.BlockSpec(memory_space=pltpu.SMEM)] + [hbm] * 8,
            out_specs=(hbm,) * 5,
            scratch_shapes=[
                pltpu.VMEM(amplitude.shape[2:], F32),
                pltpu.VMEM((positions.shape[2], 1, S), jnp.int32),
                pltpu.VMEM((2, 2, M, M), BF16),
                pltpu.VMEM((tick_cells + G + 1,) + cell, BF16),
                pltpu.VMEM((tick_cells + G + 1,) + cell, BF16),
                pltpu.VMEM((2 * G, 2, R, K), BF16),
                pltpu.VMEM((tick_cells,) + cell, BF16),
                pltpu.VMEM((tick_cells,) + cell, BF16),
                pltpu.VMEM((G,) + cell, BF16),
                pltpu.VMEM((4 * G + 1,) + cell, BF16),
                pltpu.VMEM((n_relay,) + cell, BF16),
                pltpu.VMEM((G, 2, R, K), BF16),
                pltpu.VMEM((G, 2, R, K), BF16),
                pltpu.VMEM((G,) + cell, F32),
                pltpu.VMEM((S, S), F32),
                pltpu.VMEM((TICKS, S, 8), F32),
                dma((2,)),
                dma((4,)),
                dma((2 * G,)),
                dma((tick_cells + G,)),
                dma((tick_cells + G,)),
                dma((tick_cells,)),
                dma((tick_cells,)),
                dma((n_relay,)),
                dma((n_relay,)),
                dma((4 * G,)),
                dma((4 * G,)),
                dma((2 * G,)),
                dma((2 * G,)),
                dma((5 * G,)),
            ],
            compiler_params=pltpu.CompilerParams(
                collective_id=0, has_side_effects=True, vmem_limit_bytes=60 * 1024 * 1024
            ),
        )(plan, amplitude, jnp.swapaxes(positions, 1, 2), west, north, now, nxt, east_map, south_map)

    wide = P("gx", "gy", None, None, None)
    return jax.shard_map(
        step,
        mesh=mesh,
        in_specs=(P(), wide, P("gx", "gy", None, None)) + (wide,) * 6,
        out_specs=(wide,) * 5,
        check_vma=False,
    )
```

```python
import functools

import jax
import jax.numpy as jnp
from jax import lax
from jax.experimental import pallas as pl
from jax.experimental.pallas import tpu as pltpu
from jax.sharding import PartitionSpec as P

MESH = pl.DeviceIdType.MESH
TICKS = 6
GROUPS = 4
LAG = 2
BF16 = jnp.bfloat16
F32 = jnp.float32


def kernel(
    nx,
    ny,
    plan_hbm,
    amp_hbm,
    pos_hbm,
    west_hbm,
    north_hbm,
    now_hbm,
    next_hbm,
    east_hbm,
    south_hbm,
    west_out,
    north_out,
    first_out,
    second_out,
    resid_out,
    plan,
    amp,
    pos,
    maps,
    wbuf,
    nbuf,
    cbuf,
    ebuf,
    fbuf,
    qbuf,
    rbuf,
    relay,
    rows_s,
    cols_s,
    small_sem,
    map_sem,
    c_sem,
    w_sem,
    n_sem,
    es_sem,
    fs_sem,
    rl_sem,
    rs_sem,
    q_send,
    q_recv,
    k_send,
    k_recv,
):
    gx = lax.axis_index("gx")
    gy = lax.axis_index("gy")
    G = GROUPS
    R = west_hbm.shape[3] // G
    M = west_hbm.shape[4]
    K = now_hbm.shape[4]
    NC = min(256, M)
    half = nx // 2
    has_w = gx > 0
    has_e = gx < nx - 1
    has_n = gy > 0
    has_s = gy < ny - 1
    east = (gx + 1, gy)
    west = (gx - 1, gy)
    south = (gx, gy + 1)
    north = (gx, gy - 1)
    giver = gx == half - 1
    taker = gx == half
    hubs = (gx == 0, gx == 1)
    hub_devs = ((0, gy), (1, gy))
    hub = hubs[0] | hubs[1]
    giver_dev = (half - 1, gy)
    taker_dev = (half, gy)
    core = gy % 2

    def way(it):
        return (it + core) % 3

    def straight(it):
        return has_e & jnp.logical_not(giver & (way(it) > 0))

    def relays(it):
        return (hubs[0] & (way(it) == 1)) | (hubs[1] & (way(it) == 2))

    barrier = pltpu.get_barrier_semaphore()
    partners = (
        (has_e, east),
        (has_w, west),
        (has_s, south),
        (has_n, north),
        (giver, hub_devs[0]),
        (giver, hub_devs[1]),
        (hub, giver_dev),
        (hub, taker_dev),
        (taker, hub_devs[0]),
        (taker, hub_devs[1]),
    )
    for cond, dev in partners:

        @pl.when(cond)
        def _():
            pl.semaphore_signal(barrier, 1, device_id=dev, device_id_type=MESH)

    amp_copy = pltpu.make_async_copy(amp_hbm.at[0, 0], amp, small_sem.at[0])
    pos_copy = pltpu.make_async_copy(pos_hbm.at[0], pos, small_sem.at[1])
    plan_copy = pltpu.make_async_copy(plan_hbm, plan, small_sem.at[2])
    plan_copy.start()
    amp_copy.start()
    pos_copy.start()

    def rows_of(g):
        return pl.ds(g * R, R)

    for g in range(G):
        pltpu.make_async_copy(west_hbm.at[0, 0, :, rows_of(g)], wbuf.at[g], w_sem.at[g]).start()
        pltpu.make_async_copy(north_hbm.at[0, 0, :, rows_of(g)], nbuf.at[g], n_sem.at[g]).start()
    corner_copies = []
    for k, ref in enumerate((now_hbm, next_hbm)):
        for g in range(G):
            corner_copies.append(
                pltpu.make_async_copy(
                    ref.at[0, 0, :, rows_of(g)], cbuf.at[k * G + g], c_sem.at[k * G + g]
                )
            )
    for c in corner_copies:
        c.start()
    map_copies = []
    for k, ref in enumerate((east_hbm, south_hbm)):
        for c in range(2):
            map_copies.append(
                pltpu.make_async_copy(ref.at[0, 0, c], maps.at[k, c], map_sem.at[k * 2 + c])
            )
    for c in map_copies:
        c.start()

    ZW = TICKS * G
    wbuf[ZW] = jnp.zeros((2, R, M), BF16)
    nbuf[ZW] = jnp.zeros((2, R, M), BF16)
    ZR = 4 * G
    rbuf[ZR] = jnp.zeros((2, R, M), BF16)

    @pl.when(gx == 0)
    def _():
        west_out[0, 0] = jnp.zeros((2, G * R, M), BF16)

    @pl.when(gy == 0)
    def _():
        north_out[0, 0] = jnp.zeros((2, G * R, M), BF16)
        first_out[0, 0] = jnp.zeros((2, G * R, K), BF16)
        second_out[0, 0] = jnp.zeros((2, G * R, K), BF16)

    rows_s[...] = jnp.zeros_like(rows_s)
    plan_copy.wait()
    amp_copy.wait()
    pos_copy.wait()
    for t in range(TICKS):
        b = plan[t - gx - gy + nx + ny - 2]
        rows_s[8 * t : 8 * t + 2, :] = amp[b]
        rows_s[8 * t + 2 : 8 * t + 3, :] = pos[b].astype(F32)
    flipped = rows_s[...].T
    for t in range(TICKS):
        cols_s[t] = flipped[:, 8 * t : 8 * t + 8]

    def w_index(t, g):
        return jnp.where((gx == 0) & (t > 0), ZW, t * G + g)

    def n_index(t, g):
        return jnp.where((gy == 0) & (t > 0), ZW, t * G + g)

    def land(ref, g):
        return ref.at[0, 0, :, pl.ds(pl.multiple_of(g * R, R), R)]

    def remote(src, dst, send, recv, dev):
        return pltpu.make_async_remote_copy(
            src, dst, send, recv, device_id=dev, device_id_type=MESH
        )

    def w_copy(it, last):
        dst = land(west_out, it % G) if last else wbuf.at[it + G]
        return remote(ebuf.at[it], dst, es_sem.at[it], w_sem.at[it + G], east)

    def hub_copy(it):
        dev = (jnp.maximum(way(it) - 1, 0), gy)
        return remote(ebuf.at[it], relay.at[it], es_sem.at[it], rl_sem.at[it], dev)

    def onward_copy(it, last):
        dst = land(west_out, it % G) if last else wbuf.at[it + G]
        return remote(relay.at[it], dst, rs_sem.at[it], w_sem.at[it + G], taker_dev)

    def n_copy(it, last):
        dst = land(north_out, it % G) if last else nbuf.at[it + G]
        return remote(fbuf.at[it], dst, fs_sem.at[it], n_sem.at[it + G], south)

    def q_copy(d, g, dev):
        k = d * G + g
        return remote(qbuf.at[g], rbuf.at[k], q_send.at[k], q_recv.at[k], dev)

    KQ = TICKS * G

    def q_hub_copy(g):
        k = KQ + g
        dev = (jnp.maximum(way(k) - 1, 0), gy)
        return remote(qbuf.at[g], relay.at[k], q_send.at[3 * G + g], rl_sem.at[k], dev)

    def q_onward_copy(g):
        k = KQ + g
        return remote(
            relay.at[k], rbuf.at[3 * G + g], rs_sem.at[k], q_recv.at[3 * G + g], taker_dev
        )

    def first_copy(g):
        src = wbuf.at[w_index(TICKS - 1, g), :, :, pl.ds(0, K)]
        return remote(src, land(first_out, g), k_send.at[g], k_recv.at[g], south)

    def second_copy(g):
        src = west_out.at[0, 0, :, pl.ds(g * R, R), pl.ds(0, K)]
        return remote(src, land(second_out, g), k_send.at[G + g], k_recv.at[G + g], south)

    def either(last, make, act):
        @pl.when(last)
        def _():
            getattr(make(True), act)()

        @pl.when(jnp.logical_not(last))
        def _():
            getattr(make(False), act)()

    lanes = lax.broadcasted_iota(jnp.int32, (R, NC), 1).astype(F32)

    def step(it, carry):
        t = it // G
        g = it % G
        last = t == TICKS - 1

        @pl.when(t == 0)
        def _():
            pltpu.make_async_copy(
                west_hbm.at[0, 0, :, pl.ds(pl.multiple_of(g * R, R), R)], wbuf.at[g], w_sem.at[g]
            ).wait()
            pltpu.make_async_copy(
                north_hbm.at[0, 0, :, pl.ds(pl.multiple_of(g * R, R), R)], nbuf.at[g], n_sem.at[g]
            ).wait()

        @pl.when((t > 0) & has_w)
        def _():
            w_copy(it - G, False).wait_recv()

        @pl.when((t > 0) & has_n)
        def _():
            n_copy(it - G, False).wait_recv()

        @pl.when(it == 0)
        def _():
            for c in corner_copies:
                c.wait()

        wi = w_index(t, g)
        ni = n_index(t, g)
        ci = jnp.minimum(t, 1) * G + g
        cols = cols_s[t, pl.ds(pl.multiple_of(g * R, R), R), :]
        place = cols[:, 2:3]
        for n0 in range(0, M, NC):
            hit = lanes == (place - n0)
            for c in range(2):
                total = wbuf[wi, c, :, n0 : n0 + NC].astype(F32) + nbuf[
                    ni, c, :, n0 : n0 + NC
                ].astype(F32)
                total = total + jnp.where(hit, cols[:, c : c + 1], 0.0)
                if n0 < K:
                    corner = jnp.where(t < 2, cbuf[ci, c].astype(F32), 0.0)
                    qbuf[g, c, :, 0:K] = (total[:, :K] + corner).astype(BF16)
                    if NC > K:
                        qbuf[g, c, :, K:NC] = total[:, K:].astype(BF16)
                else:
                    qbuf[g, c, :, n0 : n0 + NC] = total.astype(BF16)

        def apply(which, dst, fold):
            lhs = qbuf[g].reshape(2 * R, M)
            for n0 in range(0, M, NC):
                a = jnp.dot(lhs, maps[which, 0, :, n0 : n0 + NC], preferred_element_type=F32)
                b = jnp.dot(lhs, maps[which, 1, :, n0 : n0 + NC], preferred_element_type=F32)
                parts = (a[:R] - b[R:], b[:R] + a[R:])
                for c in range(2):
                    part = parts[c]
                    if fold and n0 < K:
                        carried = jnp.where(
                            (t > 0) & (t < TICKS - 1), wbuf[wi, c, :, 0:K].astype(F32), 0.0
                        )
                        dst[it, c, :, 0:K] = (part[:, :K] + carried).astype(BF16)
                        if NC > K:
                            dst[it, c, :, K:NC] = part[:, K:].astype(BF16)
                    else:
                        dst[it, c, :, n0 : n0 + NC] = part.astype(BF16)

        @pl.when(it == 0)
        def _():
            map_copies[0].wait()
            map_copies[1].wait()

        apply(0, ebuf, False)

        @pl.when(it == 0)
        def _():
            count = sum(cond.astype(jnp.int32) for cond, _ in partners)
            pl.semaphore_wait(barrier, count)
            map_copies[2].wait()
            map_copies[3].wait()

        @pl.when(straight(it))
        def _():
            either(last, functools.partial(w_copy, it), "start")

        @pl.when(giver & (way(it) > 0))
        def _():
            hub_copy(it).start()

        @pl.when(last)
        def _():
            @pl.when(has_s)
            def _():
                first_copy(g).start()
                q_copy(2, g, south).start()

            @pl.when(has_w)
            def _():
                q_copy(0, g, west).start()

            @pl.when(has_n)
            def _():
                q_copy(1, g, north).start()

        apply(1, fbuf, True)

        @pl.when(has_s)
        def _():
            either(last, functools.partial(n_copy, it), "start")

        back = it - LAG

        @pl.when((back >= 0) & relays(back))
        def _():
            hub_copy(back).wait_recv()
            either(back // G == TICKS - 1, functools.partial(onward_copy, back), "start")

        return carry

    lax.fori_loop(0, TICKS * G, step, 0)

    for g in range(G):

        @pl.when(giver & (way(KQ + g) > 0))
        def _():
            q_hub_copy(g).start()

        @pl.when(straight(KQ + g))
        def _():
            q_copy(3, g, east).start()

    for back in range(KQ - LAG, KQ):

        @pl.when(relays(back))
        def _():
            hub_copy(back).wait_recv()
            onward_copy(back, True).start()

    for g in range(G):

        @pl.when(relays(KQ + g))
        def _():
            q_hub_copy(g).wait_recv()
            q_onward_copy(g).start()

    for g in range(G):

        @pl.when(has_w)
        def _():
            w_copy(KQ - G + g, True).wait_recv()

        @pl.when(has_s)
        def _():
            second_copy(g).start()

    for g in range(G):
        sides = ((has_e, 0, west), (has_s, 1, north), (has_n, 2, south), (has_w, 3, east))
        for cond, d, dev in sides:

            @pl.when(cond)
            def _():
                q_copy(d, g, dev).wait_recv()

        idx = [jnp.where(cond, d * G + g, ZR) for cond, d, _ in sides]
        for n0 in range(0, M, NC):
            cut = slice(n0, n0 + NC)
            for c in range(2):
                value = 4.0 * qbuf[g, c, :, cut].astype(F32)
                for i in (3, 0, 2, 1):
                    value = value - rbuf[idx[i], c, :, cut].astype(F32)
                resid_out[0, 0, c, g * R : (g + 1) * R, cut] = value

    for g in range(G):

        @pl.when(has_n)
        def _():
            n_copy(KQ - G + g, True).wait_recv()
            first_copy(g).wait_recv()
            second_copy(g).wait_recv()

    def drain(it, carry):
        last = it // G == TICKS - 1

        @pl.when(straight(it))
        def _():
            either(last, functools.partial(w_copy, it), "wait_send")

        @pl.when(giver & (way(it) > 0))
        def _():
            hub_copy(it).wait_send()

        @pl.when(has_s)
        def _():
            either(last, functools.partial(n_copy, it), "wait_send")

        @pl.when(relays(it))
        def _():
            either(last, functools.partial(onward_copy, it), "wait_send")

        return carry

    lax.fori_loop(0, TICKS * G, drain, 0)
    for g in range(G):

        @pl.when(has_s)
        def _():
            first_copy(g).wait_send()
            second_copy(g).wait_send()
            q_copy(2, g, south).wait_send()

        @pl.when(has_w)
        def _():
            q_copy(0, g, west).wait_send()

        @pl.when(has_n)
        def _():
            q_copy(1, g, north).wait_send()

        @pl.when(giver & (way(KQ + g) > 0))
        def _():
            q_hub_copy(g).wait_send()

        @pl.when(relays(KQ + g))
        def _():
            q_onward_copy(g).wait_send()

        @pl.when(straight(KQ + g))
        def _():
            q_copy(3, g, east).wait_send()


def write_out(*refs):
    copies = [pltpu.make_async_copy(refs[k], refs[5 + k], refs[10].at[k]) for k in range(5)]
    for copy in copies:
        copy.start()
    for copy in copies:
        copy.wait()


def solution(mesh):
    nx, ny = mesh.shape["gx"], mesh.shape["gy"]

    def step(plan, amplitude, positions, west, north, now, nxt, east_map, south_map):
        G = GROUPS
        S, M = west.shape[3], west.shape[4]
        K = now.shape[4]
        R = S // G
        cell = (2, R, M)
        tick_cells = TICKS * G
        shapes = (
            (west.shape, BF16),
            (north.shape, BF16),
            (now.shape, BF16),
            (nxt.shape, BF16),
            (west.shape, F32),
        )
        out_shape = tuple(pltpu.VMEM(*each) for each in shapes)
        hbm = pl.BlockSpec(memory_space=pltpu.HBM)
        vmem = pl.BlockSpec(memory_space=pltpu.VMEM)
        dma = pltpu.SemaphoreType.DMA
        n_relay = tick_cells + G
        results = pl.pallas_call(
            functools.partial(kernel, nx, ny),
            out_shape=out_shape,
            in_specs=[hbm] * 9,
            out_specs=(vmem,) * 5,
            scratch_shapes=[
                pltpu.SMEM(plan.shape, jnp.int32),
                pltpu.VMEM(amplitude.shape[2:], F32),
                pltpu.VMEM((positions.shape[2], 1, S), jnp.int32),
                pltpu.VMEM((2, 2, M, M), BF16),
                pltpu.VMEM((tick_cells + 1,) + cell, BF16),
                pltpu.VMEM((tick_cells + 1,) + cell, BF16),
                pltpu.VMEM((2 * G, 2, R, K), BF16),
                pltpu.VMEM((tick_cells,) + cell, BF16),
                pltpu.VMEM((tick_cells,) + cell, BF16),
                pltpu.VMEM((G,) + cell, BF16),
                pltpu.VMEM((4 * G + 1,) + cell, BF16),
                pltpu.VMEM((n_relay,) + cell, BF16),
                pltpu.VMEM((S, S), F32),
                pltpu.VMEM((TICKS, S, 8), F32),
                dma((3,)),
                dma((4,)),
                dma((2 * G,)),
                dma((tick_cells + G,)),
                dma((tick_cells + G,)),
                dma((tick_cells,)),
                dma((tick_cells,)),
                dma((n_relay,)),
                dma((n_relay,)),
                dma((4 * G,)),
                dma((4 * G,)),
                dma((2 * G,)),
                dma((2 * G,)),
            ],
            compiler_params=pltpu.CompilerParams(
                collective_id=0, has_side_effects=True, vmem_limit_bytes=48 * 1024 * 1024
            ),
        )(
            *(
                pltpu.with_memory_space_constraint(x, pltpu.HBM)
                for x in (
                    plan,
                    amplitude,
                    jnp.swapaxes(positions, 1, 2),
                    west,
                    north,
                    now,
                    nxt,
                    east_map,
                    south_map,
                )
            ),
        )
        return pl.pallas_call(
            write_out,
            out_shape=tuple(jax.ShapeDtypeStruct(*each) for each in shapes),
            in_specs=[vmem] * 5,
            out_specs=(hbm,) * 5,
            scratch_shapes=[dma((5,))],
        )(*(pltpu.with_memory_space_constraint(x, pltpu.VMEM) for x in results))

    wide = P("gx", "gy", None, None, None)
    return jax.shard_map(
        step,
        mesh=mesh,
        in_specs=(P(), wide, P("gx", "gy", None, None)) + (wide,) * 6,
        out_specs=(wide,) * 5,
        check_vma=False,
    )
```

```python
import functools

import jax
import jax.numpy as jnp
from jax import lax
from jax.experimental import pallas as pl
from jax.experimental.pallas import tpu as pltpu
from jax.sharding import PartitionSpec as P

MESH = pl.DeviceIdType.MESH
TICKS = 6
GROUPS = 4
HUB_LAG = 1
BF16 = jnp.bfloat16
F32 = jnp.float32


def kernel(
    nx,
    ny,
    plan_hbm,
    amp_hbm,
    pos_hbm,
    west_hbm,
    north_hbm,
    now_hbm,
    next_hbm,
    east_hbm,
    south_hbm,
    west_out,
    north_out,
    first_out,
    second_out,
    resid_out,
    plan,
    amp,
    pos,
    maps,
    wbuf,
    nbuf,
    cbuf,
    ebuf,
    fbuf,
    qbuf,
    rbuf,
    relay,
    bent,
    rows_s,
    cols_s,
    small_sem,
    map_sem,
    c_sem,
    w_sem,
    n_sem,
    es_sem,
    fs_sem,
    rl_sem,
    rs_sem,
    bl_sem,
    bs_sem,
    q_send,
    q_recv,
    k_send,
    k_recv,
):
    gx = lax.axis_index("gx")
    gy = lax.axis_index("gy")
    G = GROUPS
    R = west_hbm.shape[3] // G
    M = west_hbm.shape[4]
    K = now_hbm.shape[4]
    NC = min(256, M)
    half = nx // 2
    has_w = gx > 0
    has_e = gx < nx - 1
    has_n = gy > 0
    has_s = gy < ny - 1
    east = (gx + 1, gy)
    west = (gx - 1, gy)
    south = (gx, gy + 1)
    north = (gx, gy - 1)
    giver = gx == half - 1
    taker = gx == half
    ender = gx == nx - 1
    hubs = (gx == 0, gx == 1)
    hub_devs = ((0, gy), (1, gy))
    hub = hubs[0] | hubs[1]
    taker_dev = (half, gy)
    core = gy % 2
    y = gx % half

    def way(it):
        return (it + core) % 3

    bends = has_e & (y < half - 1)
    stops = ((y == 3) | (y == 1), y == 3)

    def straight(it):
        return has_e & jnp.logical_not(giver & (way(it) > 0))

    def relays(it):
        return (hubs[0] & (way(it) == 1)) | (hubs[1] & (way(it) == 2))

    barrier = pltpu.get_barrier_semaphore()
    partners = (
        (has_e, east),
        (has_w, west),
        (has_s, south),
        (has_n, north),
        (y == 0, (gx + 3, gy)),
        (y == 3, (gx - 3, gy)),
        (y == 1, (gx + 2, gy)),
        (y == 3, (gx - 2, gy)),
        (ender, (half - 1, gy)),
        (giver, (nx - 1, gy)),
        (hub, taker_dev),
        (taker, hub_devs[0]),
        (taker, hub_devs[1]),
    )
    for cond, dev in partners:

        @pl.when(cond)
        def _():
            pl.semaphore_signal(barrier, 1, device_id=dev, device_id_type=MESH)

    amp_copy = pltpu.make_async_copy(amp_hbm.at[0, 0], amp, small_sem.at[0])
    pos_copy = pltpu.make_async_copy(pos_hbm.at[0], pos, small_sem.at[1])
    plan_copy = pltpu.make_async_copy(plan_hbm, plan, small_sem.at[2])
    plan_copy.start()
    amp_copy.start()
    pos_copy.start()

    def rows_of(g):
        return pl.ds(g * R, R)

    for g in range(G):
        pltpu.make_async_copy(west_hbm.at[0, 0, :, rows_of(g)], wbuf.at[g], w_sem.at[g]).start()
        pltpu.make_async_copy(north_hbm.at[0, 0, :, rows_of(g)], nbuf.at[g], n_sem.at[g]).start()
    corner_copies = []
    for k, ref in enumerate((now_hbm, next_hbm)):
        for g in range(G):
            corner_copies.append(
                pltpu.make_async_copy(
                    ref.at[0, 0, :, rows_of(g)], cbuf.at[k * G + g], c_sem.at[k * G + g]
                )
            )
    for c in corner_copies:
        c.start()
    map_copies = []
    for k, ref in enumerate((east_hbm, south_hbm)):
        for c in range(2):
            map_copies.append(
                pltpu.make_async_copy(ref.at[0, 0, c], maps.at[k, c], map_sem.at[k * 2 + c])
            )
    for c in map_copies:
        c.start()

    ZW = TICKS * G
    wbuf[ZW] = jnp.zeros((2, R, M), BF16)
    nbuf[ZW] = jnp.zeros((2, R, M), BF16)
    ZR = 4 * G
    rbuf[ZR] = jnp.zeros((2, R, M), BF16)

    @pl.when(gx == 0)
    def _():
        west_out[0, 0] = jnp.zeros((2, G * R, M), BF16)

    @pl.when(gy == 0)
    def _():
        north_out[0, 0] = jnp.zeros((2, G * R, M), BF16)
        first_out[0, 0] = jnp.zeros((2, G * R, K), BF16)
        second_out[0, 0] = jnp.zeros((2, G * R, K), BF16)

    rows_s[...] = jnp.zeros_like(rows_s)
    plan_copy.wait()
    amp_copy.wait()
    pos_copy.wait()
    for t in range(TICKS):
        b = plan[t - gx - gy + nx + ny - 2]
        rows_s[8 * t : 8 * t + 2, :] = amp[b]
        rows_s[8 * t + 2 : 8 * t + 3, :] = pos[b].astype(F32)
    flipped = rows_s[...].T
    for t in range(TICKS):
        cols_s[t] = flipped[:, 8 * t : 8 * t + 8]

    def w_index(t, g):
        return jnp.where((gx == 0) & (t > 0), ZW, t * G + g)

    def n_index(t, g):
        return jnp.where((gy == 0) & (t > 0), ZW, t * G + g)

    def land(ref, g):
        return ref.at[0, 0, :, pl.ds(pl.multiple_of(g * R, R), R)]

    def remote(src, dst, send, recv, dev):
        return pltpu.make_async_remote_copy(
            src, dst, send, recv, device_id=dev, device_id_type=MESH
        )

    def w_copy(it, last):
        k = it
        dst = land(west_out, k % G) if last else wbuf.at[k + G]
        return remote(ebuf.at[k], dst, es_sem.at[k], w_sem.at[k + G], east)

    def hub_copy(it):
        k = it
        dev = (jnp.maximum(way(it) - 1, 0), gy)
        return remote(ebuf.at[k], relay.at[k], es_sem.at[k], rl_sem.at[k], dev)

    def onward_copy(it, last):
        k = it
        dst = land(west_out, k % G) if last else wbuf.at[k + G]
        return remote(relay.at[k], dst, rs_sem.at[k], w_sem.at[k + G], taker_dev)

    def n_copy(it, last):
        k = it
        dst = land(north_out, k % G) if last else nbuf.at[k + G]
        return remote(fbuf.at[k], dst, fs_sem.at[k], n_sem.at[k + G], south)

    def w_recv(k, last):
        dst = land(west_out, k % G) if last else wbuf.at[k]
        return remote(ebuf.at[0], dst, es_sem.at[0], w_sem.at[k], east)

    def n_recv(k, last):
        dst = land(north_out, k % G) if last else nbuf.at[k]
        return remote(fbuf.at[0], dst, fs_sem.at[0], n_sem.at[k], south)

    def q_copy(d, g, dev):
        k = d * G + g
        return remote(qbuf.at[g], rbuf.at[k], q_send.at[k], q_recv.at[k], dev)

    KQ = TICKS * G

    def q_hub_copy(g):
        k = KQ + g
        dev = (jnp.maximum(way(k) - 1, 0), gy)
        return remote(qbuf.at[g], relay.at[k], q_send.at[3 * G + g], rl_sem.at[k], dev)

    def q_onward_copy(g):
        k = KQ + g
        return remote(
            relay.at[k], rbuf.at[3 * G + g], rs_sem.at[k], q_recv.at[3 * G + g], taker_dev
        )

    def q_back_copy(g):
        k = KQ + g
        return remote(qbuf.at[g], relay.at[k], q_send.at[g], rl_sem.at[k], (nx - 1, gy))

    def q_return_copy(g):
        k = KQ + g
        return remote(relay.at[k], rbuf.at[g], rs_sem.at[k], q_recv.at[g], (half - 1, gy))

    def q_bend_copy():
        d = jnp.where(y == 1, 1, 0)
        dev = (jnp.where(y < 2, gx - y + 3, gx - 1), gy)
        return remote(qbuf.at[0], bent.at[d], q_send.at[3 * G], bl_sem.at[d], dev)

    def q_unbend_copy(kind):
        dev = (jnp.where(y == 1, gx + 2, gx - 2 + kind), gy)
        return remote(bent.at[kind], rbuf.at[3 * G], bs_sem.at[kind], q_recv.at[3 * G], dev)

    def q_bend_recv(kind):
        return remote(qbuf.at[0], bent.at[kind], q_send.at[3 * G], bl_sem.at[kind], east)

    def first_copy(g):
        src = wbuf.at[w_index(TICKS - 1, g), :, :, pl.ds(0, K)]
        return remote(src, land(first_out, g), k_send.at[g], k_recv.at[g], south)

    def second_copy(g):
        src = west_out.at[0, 0, :, pl.ds(g * R, R), pl.ds(0, K)]
        return remote(src, land(second_out, g), k_send.at[G + g], k_recv.at[G + g], south)

    def either(last, make, act):
        @pl.when(last)
        def _():
            getattr(make(True), act)()

        @pl.when(jnp.logical_not(last))
        def _():
            getattr(make(False), act)()

    lanes = lax.broadcasted_iota(jnp.int32, (R, NC), 1).astype(F32)

    def step(it, carry):
        t = it // G
        g = it % G
        last = t == TICKS - 1

        @pl.when(t == 0)
        def _():
            pltpu.make_async_copy(
                west_hbm.at[0, 0, :, pl.ds(pl.multiple_of(g * R, R), R)], wbuf.at[g], w_sem.at[g]
            ).wait()
            pltpu.make_async_copy(
                north_hbm.at[0, 0, :, pl.ds(pl.multiple_of(g * R, R), R)], nbuf.at[g], n_sem.at[g]
            ).wait()

        @pl.when((t > 0) & has_w)
        def _():
            w_recv(it, False).wait_recv()

        @pl.when((t > 0) & has_n)
        def _():
            n_recv(it, False).wait_recv()

        @pl.when(it == 0)
        def _():
            for c in corner_copies:
                c.wait()

        wi = w_index(t, g)
        ni = n_index(t, g)
        ci = jnp.minimum(t, 1) * G + g
        cols = cols_s[t, pl.ds(pl.multiple_of(g * R, R), R), :]
        place = cols[:, 2:3]
        for n0 in range(0, M, NC):
            hit = lanes == (place - n0)
            for c in range(2):
                total = wbuf[wi, c, :, n0 : n0 + NC].astype(F32) + nbuf[
                    ni, c, :, n0 : n0 + NC
                ].astype(F32)
                total = total + jnp.where(hit, cols[:, c : c + 1], 0.0)
                if n0 < K:
                    corner = jnp.where(t < 2, cbuf[ci, c].astype(F32), 0.0)
                    qbuf[g, c, :, 0:K] = (total[:, :K] + corner).astype(BF16)
                    if NC > K:
                        qbuf[g, c, :, K:NC] = total[:, K:].astype(BF16)
                else:
                    qbuf[g, c, :, n0 : n0 + NC] = total.astype(BF16)

        def apply(which, dst, fold):
            lhs = qbuf[g].reshape(2 * R, M)
            for n0 in range(0, M, NC):
                a = jnp.dot(lhs, maps[which, 0, :, n0 : n0 + NC], preferred_element_type=F32)
                b = jnp.dot(lhs, maps[which, 1, :, n0 : n0 + NC], preferred_element_type=F32)
                parts = (a[:R] - b[R:], b[:R] + a[R:])
                for c in range(2):
                    part = parts[c]
                    if fold and n0 < K:
                        carried = jnp.where(
                            (t > 0) & (t < TICKS - 1), wbuf[wi, c, :, 0:K].astype(F32), 0.0
                        )
                        dst[it, c, :, 0:K] = (part[:, :K] + carried).astype(BF16)
                        if NC > K:
                            dst[it, c, :, K:NC] = part[:, K:].astype(BF16)
                    else:
                        dst[it, c, :, n0 : n0 + NC] = part.astype(BF16)

        @pl.when(it == 0)
        def _():
            map_copies[0].wait()
            map_copies[1].wait()

        apply(0, ebuf, False)

        @pl.when(it == 0)
        def _():
            count = sum(cond.astype(jnp.int32) for cond, _ in partners)
            pl.semaphore_wait(barrier, count)
            map_copies[2].wait()
            map_copies[3].wait()

        @pl.when(straight(it) & jnp.logical_not(giver))
        def _():
            either(last, functools.partial(w_copy, it), "start")

        @pl.when(giver & (way(it) > 0))
        def _():
            hub_copy(it).start()

        @pl.when(last)
        def _():
            @pl.when(has_s)
            def _():
                first_copy(g).start()
                q_copy(2, g, south).start()

            @pl.when(has_w & jnp.logical_not(taker & (g % 2 == 1)))
            def _():
                q_copy(0, g, west).start()

            @pl.when(taker & (g % 2 == 1))
            def _():
                q_back_copy(g).start()

            @pl.when(bends & (g == 0))
            def _():
                q_bend_copy().start()

            @pl.when(has_n)
            def _():
                q_copy(1, g, north).start()

        apply(1, fbuf, True)

        @pl.when(has_s)
        def _():
            either(last, functools.partial(n_copy, it), "start")

        @pl.when(straight(it) & giver)
        def _():
            either(last, functools.partial(w_copy, it), "start")

        back = it - HUB_LAG

        @pl.when((back >= 0) & relays(back))
        def _():
            hub_copy(back).wait_recv()
            either(back // G == TICKS - 1, functools.partial(onward_copy, back), "start")

        return carry

    lax.fori_loop(0, TICKS * G, step, 0)

    for g in range(G):

        @pl.when(giver & (way(KQ + g) > 0))
        def _():
            q_hub_copy(g).start()

        @pl.when(straight(KQ + g) & (jnp.logical_not(bends) if g == 0 else True))
        def _():
            q_copy(3, g, east).start()

    for kind in range(2):

        @pl.when(stops[kind])
        def _():
            q_bend_recv(kind).wait_recv()
            q_unbend_copy(kind).start()

    for back in range(KQ - HUB_LAG, KQ):

        @pl.when(relays(back))
        def _():
            hub_copy(back).wait_recv()
            onward_copy(back, True).start()

    for g in range(G):

        @pl.when(relays(KQ + g))
        def _():
            q_hub_copy(g).wait_recv()
            q_onward_copy(g).start()

        if g % 2 == 1:

            @pl.when(ender)
            def _():
                q_back_copy(g).wait_recv()
                q_return_copy(g).start()

    for g in range(G):

        @pl.when(has_w)
        def _():
            w_recv(KQ + g, True).wait_recv()

        @pl.when(has_s)
        def _():
            second_copy(g).start()

    for g in range(G):
        sides = ((has_e, 0, west), (has_s, 1, north), (has_n, 2, south), (has_w, 3, east))
        for cond, d, dev in sides:

            @pl.when(cond)
            def _():
                q_copy(d, g, dev).wait_recv()

        idx = [jnp.where(cond, d * G + g, ZR) for cond, d, _ in sides]
        for n0 in range(0, M, NC):
            cut = slice(n0, n0 + NC)
            for c in range(2):
                value = 4.0 * qbuf[g, c, :, cut].astype(F32)
                for i in (3, 0, 2, 1):
                    value = value - rbuf[idx[i], c, :, cut].astype(F32)
                resid_out[0, 0, c, g * R : (g + 1) * R, cut] = value

    for g in range(G):

        @pl.when(has_n)
        def _():
            n_recv(KQ + g, True).wait_recv()
            first_copy(g).wait_recv()
            second_copy(g).wait_recv()

    def drain(it, carry):
        last = it // G == TICKS - 1

        @pl.when(straight(it))
        def _():
            either(last, functools.partial(w_copy, it), "wait_send")

        @pl.when(giver & (way(it) > 0))
        def _():
            hub_copy(it).wait_send()

        @pl.when(has_s)
        def _():
            either(last, functools.partial(n_copy, it), "wait_send")

        @pl.when(relays(it))
        def _():
            either(last, functools.partial(onward_copy, it), "wait_send")

        return carry

    lax.fori_loop(0, TICKS * G, drain, 0)
    for g in range(G):

        @pl.when(has_s)
        def _():
            first_copy(g).wait_send()
            second_copy(g).wait_send()
            q_copy(2, g, south).wait_send()

        @pl.when(has_w)
        def _():
            q_copy(0, g, west).wait_send()

        if g % 2 == 1:

            @pl.when(ender)
            def _():
                q_return_copy(g).wait_send()

        @pl.when(has_n)
        def _():
            q_copy(1, g, north).wait_send()

        @pl.when(giver & (way(KQ + g) > 0))
        def _():
            q_hub_copy(g).wait_send()

        @pl.when(relays(KQ + g))
        def _():
            q_onward_copy(g).wait_send()

        @pl.when(straight(KQ + g))
        def _():
            q_copy(3, g, east).wait_send()

    for kind in range(2):

        @pl.when(stops[kind])
        def _():
            q_unbend_copy(kind).wait_send()


def write_out(*refs):
    copies = [pltpu.make_async_copy(refs[k], refs[5 + k], refs[10].at[k]) for k in range(5)]
    for copy in copies:
        copy.start()
    for copy in copies:
        copy.wait()


def solution(mesh):
    nx, ny = mesh.shape["gx"], mesh.shape["gy"]

    def step(plan, amplitude, positions, west, north, now, nxt, east_map, south_map):
        G = GROUPS
        S, M = west.shape[3], west.shape[4]
        K = now.shape[4]
        R = S // G
        cell = (2, R, M)
        tick_cells = TICKS * G
        shapes = (
            (west.shape, BF16),
            (north.shape, BF16),
            (now.shape, BF16),
            (nxt.shape, BF16),
            (west.shape, F32),
        )
        out_shape = tuple(pltpu.VMEM(*each) for each in shapes)
        hbm = pl.BlockSpec(memory_space=pltpu.HBM)
        vmem = pl.BlockSpec(memory_space=pltpu.VMEM)
        dma = pltpu.SemaphoreType.DMA
        n_relay = tick_cells + G
        results = pl.pallas_call(
            functools.partial(kernel, nx, ny),
            out_shape=out_shape,
            in_specs=[hbm] * 9,
            out_specs=(vmem,) * 5,
            scratch_shapes=[
                pltpu.SMEM(plan.shape, jnp.int32),
                pltpu.VMEM(amplitude.shape[2:], F32),
                pltpu.VMEM((positions.shape[2], 1, S), jnp.int32),
                pltpu.VMEM((2, 2, M, M), BF16),
                pltpu.VMEM((tick_cells + 1,) + cell, BF16),
                pltpu.VMEM((tick_cells + 1,) + cell, BF16),
                pltpu.VMEM((2 * G, 2, R, K), BF16),
                pltpu.VMEM((tick_cells,) + cell, BF16),
                pltpu.VMEM((tick_cells,) + cell, BF16),
                pltpu.VMEM((G,) + cell, BF16),
                pltpu.VMEM((4 * G + 1,) + cell, BF16),
                pltpu.VMEM((n_relay,) + cell, BF16),
                pltpu.VMEM((2,) + cell, BF16),
                pltpu.VMEM((S, S), F32),
                pltpu.VMEM((TICKS, S, 8), F32),
                dma((3,)),
                dma((4,)),
                dma((2 * G,)),
                dma((tick_cells + G,)),
                dma((tick_cells + G,)),
                dma((tick_cells,)),
                dma((tick_cells,)),
                dma((n_relay,)),
                dma((n_relay,)),
                dma((2,)),
                dma((2,)),
                dma((4 * G,)),
                dma((4 * G,)),
                dma((2 * G,)),
                dma((2 * G,)),
            ],
            compiler_params=pltpu.CompilerParams(
                collective_id=0, has_side_effects=True, vmem_limit_bytes=48 * 1024 * 1024
            ),
        )(
            *(
                pltpu.with_memory_space_constraint(x, pltpu.HBM)
                for x in (
                    plan,
                    amplitude,
                    jnp.swapaxes(positions, 1, 2),
                    west,
                    north,
                    now,
                    nxt,
                    east_map,
                    south_map,
                )
            ),
        )
        return pl.pallas_call(
            write_out,
            out_shape=tuple(jax.ShapeDtypeStruct(*each) for each in shapes),
            in_specs=[vmem] * 5,
            out_specs=(hbm,) * 5,
            scratch_shapes=[dma((5,))],
        )(*(pltpu.with_memory_space_constraint(x, pltpu.VMEM) for x in results))

    wide = P("gx", "gy", None, None, None)
    return jax.shard_map(
        step,
        mesh=mesh,
        in_specs=(P(), wide, P("gx", "gy", None, None)) + (wide,) * 6,
        out_specs=(wide,) * 5,
        check_vma=False,
    )
```
